32 devices in a mesh: fsdp: 8 (over z, x), ctx: 4 (over y, core).
Axes of the slice: x: 2, y: 2, z: 4, core: 2. Of those that a mesh axis runs over, the one named last changes fastest.
Arguments:
- inputs: bfloat16 [4096, 768], P(('fsdp', 'ctx')), may hold values from -6 to 6
- lengths: int32 [8, 3], P('fsdp'), may hold values from 1 to 384, 512 in all within a row
- norm1_gain: bfloat16 [768], P(('fsdp', 'ctx')), may hold values from 0.5 to 1.5
- qkv_weight: bfloat16 [768, 2304], P(('fsdp', 'ctx'))
- attn_out_weight: bfloat16 [768, 768], P(('fsdp', 'ctx')), may hold values from -2.5 to 2.5
- norm2_gain: bfloat16 [768], P(('fsdp', 'ctx')), may hold values from 0.5 to 1.5
- ffn_in_weight: bfloat16 [768, 2304], P(('fsdp', 'ctx')), may hold values from -0.21875 to 0.21875
- ffn_out_weight: bfloat16 [1152, 768], P(None, ('fsdp', 'ctx')), may hold values from -0.1875 to 0.1875
- out_grad: bfloat16 [4096, 768], P(('fsdp', 'ctx')), may hold values from -6 to 6
Outputs:
- outputs: bfloat16 [4096, 768], P(('fsdp', 'ctx'))
- input_grad: bfloat16 [4096, 768], P(('fsdp', 'ctx'))
- norm1_gain_grad: float32 [768], P(('fsdp', 'ctx'))
- qkv_weight_grad: float32 [768, 2304], P(('fsdp', 'ctx'))
- attn_out_weight_grad: float32 [768, 768], P(('fsdp', 'ctx'))
- norm2_gain_grad: float32 [768], P(('fsdp', 'ctx'))
- ffn_in_weight_grad: float32 [768, 2304], P(('fsdp', 'ctx'))
- ffn_out_weight_grad: float32 [1152, 768], P(None, ('fsdp', 'ctx'))
The draws below stay inside these ranges and needn't reach their ends.
Inputs may be any that keep to these rules, and one draw needn't show every extreme that they name: `lengths`: each row sums to 512, and its largest entry is exactly 384.
All inputs are finite; a program needn't handle non-finite values.
Results may differ from the reference program's by a relative error of at most 0.038.
The reference program's roundings to bfloat16 on the way count: a program that leaves them out, or rounds other values in their place, can miss the bound.
Values may be sent and summed in bfloat16 or wider, within the bound.
No kernel may reach another device: no remote copies, remote signals or barrier semaphores. Data moves between devices by JAX's collectives and lax.ppermute only.
A program may use at most 128 MiB of HBM per device.

```python
import math
import jax
import jax.numpy as jnp
import numpy as np
from jax import lax

D = 768
HEADS = 12
HEAD_DIM = 64
FF = 1152
SEQ_GRP = 3
GROUP = 512
MAXLEN = 384
TOKENS = 4096
N_FSDP = 8


def draw_qkv_weight(key, part):
    drawn_base = jax.random.normal(key, (D, 3 * D), jnp.float32) * D ** (-0.5)
    return drawn_base.astype(jnp.bfloat16)


def strengthened(drawn, rng, source, target, shards_of, factor):
    def block_of(dim):
        return (jnp.arange(drawn.shape[dim]) // (drawn.shape[dim] // shards_of)).reshape((-1,) + (1,) * (drawn.ndim - 1 - dim))

    near = jax.random.permutation(rng, shards_of)[block_of(target)]
    far = (block_of(target) + shards_of // 2) % shards_of
    return jnp.where((block_of(source) == near) | (block_of(source) == far), factor * drawn, drawn)


def levels(rng, extent, pieces, low, largest):
    level, own = 1.0, jax.random.fold_in(rng, 6)
    for axis_at, parts in pieces:
        steps = jnp.exp(jax.random.uniform(jax.random.fold_in(own, axis_at), (parts,), jnp.float32, low / len(pieces), largest / len(pieces)))
        level = level * jnp.repeat(steps, extent[axis_at] // parts).reshape([-1 if axis == axis_at else 1 for axis in range(len(extent))])
    return level


def length_profile(count, total, most, lean):
    weights = [(1 << 20) // math.isqrt(rank ** lean) + 1 for rank in range(2, count + 1)]
    spare, counts = total - most - (count - 1), [1] * (count - 1)
    while spare > 0:
        movable = [i for i in range(count - 1) if counts[i] < most]
        mass, left = sum([weights[i] for i in movable]), spare
        for i in movable:
            more = min(most - counts[i], max(1, left * weights[i] // mass), spare)
            counts[i] = counts[i] + more
            spare = spare - more
    return np.array([most] + counts)


def ragged(stream_key, count, total, limit, slope):
    if count == 2:
        one = jax.random.randint(stream_key, (), max(1, total - limit), min(limit, total - 1) + 1)
        return jnp.stack([one, total - one])
    tallies = jnp.asarray(length_profile(count, total, limit, slope), jnp.int32)
    couples = (count - 1) // 2
    source_of, receiver = tallies[1:1 + 2 * couples:2], tallies[2:2 + 2 * couples:2]
    margin = jnp.minimum(source_of - 1, limit - receiver)
    passed = jax.random.randint(jax.random.fold_in(stream_key, 1), (couples,), 0, 1 << 20) % (margin + 1)
    tallies = tallies.at[1:1 + 2 * couples:2].set(source_of - passed).at[2:2 + 2 * couples:2].set(receiver + passed)
    return tallies[jax.random.permutation(jax.random.fold_in(stream_key, 2), count)]


def bell_draw(own_key, dims, scale, most, shards=(), kind=jnp.bfloat16):
    drawn = jax.random.normal(own_key, dims, jnp.float32) * scale
    if len(shards) > 0:
        drawn = levels(own_key, dims, shards, -0.22, 0.18) * drawn
    return jnp.clip(drawn, min=-most, max=most).astype(kind)


def gaussian_with(own_key, dims, deviation, limit, cuts, heavy, kind=jnp.bfloat16):
    drawn = deviation * jax.random.normal(own_key, dims, jnp.float32)
    if cuts:
        drawn = drawn * levels(own_key, dims, cuts, -0.22, 0.18)
    return jnp.clip(strengthened(drawn, jax.random.fold_in(own_key, 3), *heavy), -limit, limit).astype(kind)


def setup_inputs(seed: int = 0) -> dict:
    splits = jax.random.split(jax.random.key(seed), 10)
    inputs = bell_draw(splits[0], (TOKENS, D), 1.0, 6.0, ((0, 32),))
    lengths = jax.vmap(lambda own: ragged(own, SEQ_GRP, GROUP, MAXLEN, 2))(jax.random.split(splits[1], N_FSDP)).reshape((N_FSDP, SEQ_GRP)).astype(jnp.int32)
    norm1_gain = jnp.clip(1.0 + 0.1 * jax.random.normal(splits[2], (D,), jnp.float32), 0.5, 1.5).astype(jnp.bfloat16)
    qkv_weight = draw_qkv_weight(jax.random.fold_in(splits[9], 71), 0)
    attn_out_weight = bell_draw(splits[4], (D, D), (D // 128) ** -0.5, 2.5, ((0, 32),))
    norm2_gain = jnp.clip(1.0 + 0.1 * jax.random.normal(splits[5], (D,), jnp.float32), 0.5, 1.5).astype(jnp.bfloat16)
    ffn_in_weight = bell_draw(splits[6], (D, 2 * FF), D ** -0.5, 0.21875, ((0, 32),))
    ffn_out_weight = bell_draw(splits[7], (FF, D), FF ** -0.5, 0.1875, ((1, 32),))
    out_grad = gaussian_with(splits[8], (TOKENS, D), 1.0, 6.0, ((0, 32),), (0, 1, 32, 2.75))
    return {"inputs": inputs, "lengths": lengths, "norm1_gain": norm1_gain, "qkv_weight": qkv_weight, "attn_out_weight": attn_out_weight, "norm2_gain": norm2_gain, "ffn_in_weight": ffn_in_weight, "ffn_out_weight": ffn_out_weight, "out_grad": out_grad}


rope_base = 160000.0
norm_eps = 1e-05
score_scale = 0.125

def positions(length_row, index_rows):
    seq_ends = jnp.cumsum(length_row).astype(jnp.int32)
    starts = (seq_ends - length_row).astype(jnp.int32)
    segment = lax.optimization_barrier(jnp.sum((index_rows[:, None] >= seq_ends[None, :]).astype(jnp.int32), axis=1))
    seq_numbers = jnp.arange(length_row.shape[0], dtype=jnp.int32)
    seq_start = lax.optimization_barrier(jnp.sum(jnp.where(segment[:, None] == seq_numbers[None, :], starts[None, :], 0), axis=1))
    return (segment.astype(jnp.int32), (index_rows - seq_start).astype(jnp.int32))

def rope_tables(places):
    freq_steps = jnp.arange(32, dtype=jnp.float32)
    frequency = jnp.exp(freq_steps * (-2.0 / 64.0) * math.log(rope_base))
    angles = places.astype(jnp.float32)[:, None] * frequency[None, :]
    angles = jnp.concatenate([angles, angles], axis=1)
    return (jnp.cos(angles), jnp.sin(angles))

def rotate(values_in, cosine, sine_tab):
    half_width = values_in.shape[-1] // 2
    turned = jnp.concatenate([-values_in[..., half_width:], values_in[..., :half_width]], axis=-1)
    return values_in * cosine[:, None, :] + turned * sine_tab[:, None, :]

def unrotate(values_in, cosine, sine_tab):
    half_width = values_in.shape[-1] // 2
    scaled = values_in * sine_tab[:, None, :]
    turned_back = jnp.concatenate([scaled[..., half_width:], -scaled[..., :half_width]], axis=-1)
    return values_in * cosine[:, None, :] + turned_back

def layer_norm(values_in):
    average = lax.optimization_barrier(jnp.mean(values_in, axis=-1, keepdims=True))
    centred = values_in - average
    spread = lax.optimization_barrier(jnp.mean(centred * centred, axis=-1, keepdims=True))
    inv_scale = lax.rsqrt(spread + norm_eps)
    return (centred * inv_scale, inv_scale)

def norm_back(grad_h, normed, inv_scale, gain_row):
    grad_n = grad_h * gain_row
    return inv_scale * (grad_n - lax.optimization_barrier(jnp.mean(grad_n, axis=-1, keepdims=True)) - normed * lax.optimization_barrier(jnp.mean(grad_n * normed, axis=-1, keepdims=True)))

def gelu_parts(gate_in):
    normal_cdf = 0.5 * (1.0 + lax.erf(gate_in * (1.0 / math.sqrt(2.0))))
    normal_pdf = jnp.exp(-0.5 * gate_in * gate_in) * (1.0 / math.sqrt(2.0 * math.pi))
    return (gate_in * normal_cdf, normal_cdf + gate_in * normal_pdf)

def layer_pass(params, block_in, length_row, block_grad):
    gain_one, w_qkv, w_attn, gain_two, w_in, w_out = params
    f32 = jnp.float32
    bf16 = jnp.bfloat16
    index_rows = jnp.arange(GROUP, dtype=jnp.int32)
    segment, places = positions(length_row, index_rows)
    cosine, sine_tab = rope_tables(places)
    resid_in = block_in.astype(f32)
    normed_one, scale_one = layer_norm(resid_in)
    hidden_one = (normed_one * gain_one.astype(f32)).astype(bf16)
    joined_out = jnp.dot(hidden_one, w_qkv, preferred_element_type=f32)
    queries = rotate(joined_out[:, :D].reshape(GROUP, HEADS, HEAD_DIM), cosine, sine_tab).astype(bf16)
    key_rows = rotate(joined_out[:, D:2 * D].reshape(GROUP, HEADS, HEAD_DIM), cosine, sine_tab).astype(bf16)
    value_rows = joined_out[:, 2 * D:].reshape(GROUP, HEADS, HEAD_DIM).astype(bf16)
    query_f = queries.astype(f32)
    key_f = key_rows.astype(f32)
    value_f = value_rows.astype(f32)
    scores = jnp.einsum('thd,uhd->htu', query_f, key_f) * score_scale
    allowed = segment[:, None] == segment[None, :]
    scores = jnp.where(allowed[None, :, :], scores, -1e+30)
    row_top = lax.optimization_barrier(jnp.max(scores, axis=2, keepdims=True))
    logsum = row_top + jnp.log(lax.optimization_barrier(jnp.sum(jnp.exp(scores - row_top), axis=2, keepdims=True)))
    prob_full = jnp.exp(scores - logsum)
    prob_half = prob_full.astype(bf16)
    attended = jnp.einsum('htu,uhd->thd', prob_half.astype(f32), value_f).astype(bf16).reshape(GROUP, D)
    resid_mid = resid_in + jnp.dot(attended, w_attn, preferred_element_type=f32)
    normed_two, scale_two = layer_norm(resid_mid)
    hidden_two = (normed_two * gain_two.astype(f32)).astype(bf16)
    expanded = jnp.dot(hidden_two, w_in, preferred_element_type=f32)
    gate_in = expanded[:, :FF]
    up_in = expanded[:, FF:]
    activated, gelu_slope = gelu_parts(gate_in)
    mixed_act = (activated * up_in).astype(bf16)
    outputs = (resid_mid + jnp.dot(mixed_act, w_out, preferred_element_type=f32)).astype(bf16)
    grad_w_out = jnp.dot(mixed_act.T, block_grad, preferred_element_type=f32)
    grad_mixed = jnp.dot(block_grad, w_out.T, preferred_element_type=f32)
    grad_expanded = jnp.concatenate([grad_mixed * up_in * gelu_slope, grad_mixed * activated], axis=1).astype(bf16)
    grad_w_in = jnp.dot(hidden_two.T, grad_expanded, preferred_element_type=f32)
    grad_hidden_two = jnp.dot(grad_expanded, w_in.T, preferred_element_type=f32)
    grad_gain_two = lax.optimization_barrier(jnp.sum(grad_hidden_two * normed_two, axis=0))
    grad_mid = block_grad.astype(f32) + norm_back(grad_hidden_two, normed_two, scale_two, gain_two.astype(f32))
    grad_mid_half = grad_mid.astype(bf16)
    grad_w_attn = jnp.dot(attended.T, grad_mid_half, preferred_element_type=f32)
    grad_att = jnp.dot(grad_mid_half, w_attn.T, preferred_element_type=f32).astype(bf16)
    grad_att_f = grad_att.reshape(GROUP, HEADS, HEAD_DIM).astype(f32)
    attended_f = attended.reshape(GROUP, HEADS, HEAD_DIM).astype(f32)
    row_delta = lax.optimization_barrier(jnp.sum(grad_att_f * attended_f, axis=2)).T[:, :, None]
    grad_v = jnp.einsum('htu,thd->uhd', prob_half.astype(f32), grad_att_f).astype(bf16)
    grad_p = jnp.einsum('thd,uhd->htu', grad_att_f, value_f)
    grad_s = (prob_full * (grad_p - row_delta)).astype(bf16).astype(f32)
    grad_q = jnp.einsum('htu,uhd->thd', grad_s, key_f) * score_scale
    grad_k = jnp.einsum('htu,thd->uhd', grad_s, query_f) * score_scale
    grad_q = unrotate(grad_q, cosine, sine_tab).astype(bf16).reshape(GROUP, D)
    grad_k = unrotate(grad_k, cosine, sine_tab).astype(bf16).reshape(GROUP, D)
    grad_joined = jnp.concatenate([grad_q, grad_k, grad_v.reshape(GROUP, D)], axis=1)
    grad_w_qkv = jnp.dot(hidden_one.T, grad_joined, preferred_element_type=f32)
    grad_hidden_one = jnp.dot(grad_joined, w_qkv.T, preferred_element_type=f32)
    grad_gain_one = lax.optimization_barrier(jnp.sum(grad_hidden_one * normed_one, axis=0))
    input_grad = (grad_mid + norm_back(grad_hidden_one, normed_one, scale_one, gain_one.astype(f32))).astype(bf16)
    grads = (grad_gain_one, grad_w_qkv, grad_w_attn, grad_gain_two, grad_w_in, grad_w_out)
    return (outputs, input_grad, grads)

def reference(inputs, lengths, norm1_gain, qkv_weight, attn_out_weight, norm2_gain, ffn_in_weight, ffn_out_weight, out_grad):
    params = (norm1_gain, qkv_weight, attn_out_weight, norm2_gain, ffn_in_weight, ffn_out_weight)
    blocks_in = inputs.reshape(N_FSDP, GROUP, D)
    blocks_grad = out_grad.reshape(N_FSDP, GROUP, D)
    start_sums = tuple((jnp.zeros(p.shape, jnp.float32) for p in params))

    def step_group(carry, packed):
        block_in, length_row, block_grad = packed
        outputs, input_grad, grads = layer_pass(params, block_in, length_row, block_grad)
        carry = tuple((c + g for c, g in zip(carry, grads)))
        return (carry, (outputs, input_grad))
    sums, (outs_all, grads_all) = lax.scan(step_group, start_sums, (blocks_in, lengths, blocks_grad))
    return (outs_all.reshape(TOKENS, D), grads_all.reshape(TOKENS, D), sums[0], sums[1], sums[2], sums[3], sums[4], sums[5])
```

```python
import math

import jax
import jax.numpy as jnp
from jax import lax
from jax.sharding import PartitionSpec as P

rope_base = 160000.0
norm_eps = 1e-05
score_scale = 0.125


def positions(length_row, index_rows):
    seq_ends = jnp.cumsum(length_row)
    starts = seq_ends - length_row
    segment = jnp.sum((index_rows[:, None] >= seq_ends[None, :]).astype(jnp.int32), axis=1)
    seq_numbers = jnp.arange(length_row.shape[0], dtype=jnp.int32)
    seq_start = jnp.sum(
        jnp.where(segment[:, None] == seq_numbers[None, :], starts[None, :], 0), axis=1
    )
    return (segment, index_rows - seq_start)


def rope_tables(places):
    freq_steps = jnp.arange(32, dtype=jnp.float32)
    frequency = jnp.exp(freq_steps * (-2.0 / 64.0) * math.log(rope_base))
    angles = places.astype(jnp.float32)[:, None] * frequency[None, :]
    angles = jnp.concatenate([angles, angles], axis=1)
    return (jnp.cos(angles), jnp.sin(angles))


def rotate(values_in, cosine, sine_tab):
    half_width = values_in.shape[-1] // 2
    turned = jnp.concatenate([-values_in[..., half_width:], values_in[..., :half_width]], axis=-1)
    return values_in * cosine[:, None, :] + turned * sine_tab[:, None, :]


def unrotate(values_in, cosine, sine_tab):
    half_width = values_in.shape[-1] // 2
    scaled = values_in * sine_tab[:, None, :]
    turned_back = jnp.concatenate([scaled[..., half_width:], -scaled[..., :half_width]], axis=-1)
    return values_in * cosine[:, None, :] + turned_back


def layer_norm(values_in):
    average = jnp.mean(values_in, axis=-1, keepdims=True)
    centred = values_in - average
    spread = jnp.mean(centred * centred, axis=-1, keepdims=True)
    inv_scale = lax.rsqrt(spread + norm_eps)
    return (centred * inv_scale, inv_scale)


def norm_back(grad_h, normed, inv_scale, gain_row):
    grad_n = grad_h * gain_row
    return inv_scale * (
        grad_n
        - jnp.mean(grad_n, axis=-1, keepdims=True)
        - normed * jnp.mean(grad_n * normed, axis=-1, keepdims=True)
    )


def gelu_parts(gate_in):
    normal_cdf = 0.5 * (1.0 + lax.erf(gate_in * (1.0 / math.sqrt(2.0))))
    normal_pdf = jnp.exp(-0.5 * gate_in * gate_in) * (1.0 / math.sqrt(2.0 * math.pi))
    return (gate_in * normal_cdf, normal_cdf + gate_in * normal_pdf)


def contract_rows(left_side, right_side):
    return lax.dot_general(
        left_side, right_side, (((0,), (0,)), ((), ())), preferred_element_type=jnp.float32
    )


def contract_last(left_side, right_side):
    return lax.dot_general(
        left_side, right_side, (((1,), (1,)), ((), ())), preferred_element_type=jnp.float32
    )


def block_scores(block_query, head_keys, segment):
    scores = contract_last(block_query, head_keys) * score_scale
    allowed = segment[:, None] == segment[None, :]
    return jnp.where(allowed, scores, -1e30)


def attend(queries, key_rows, value_rows, segment, block_rows):
    head_outs = []
    head_sums = []
    for head_index in range(queries.shape[1] // 64):
        head_cols = slice(64 * head_index, 64 * head_index + 64)
        head_keys = key_rows[:, head_cols]
        head_values = value_rows[:, head_cols]
        block_query = queries[0:block_rows, head_cols]
        scores = block_scores(block_query, head_keys, segment)
        row_top = jnp.max(scores, axis=1, keepdims=True)
        logsum = row_top + jnp.log(jnp.sum(jnp.exp(scores - row_top), axis=1, keepdims=True))
        prob_block = jnp.exp(scores - logsum).astype(jnp.bfloat16)
        rows_out = jnp.dot(prob_block, head_values, preferred_element_type=jnp.float32).astype(
            jnp.bfloat16
        )
        rows_sum = logsum[:, 0]
        head_outs.append(rows_out)
        head_sums.append(rows_sum)
    return (jnp.concatenate(head_outs, axis=1), jnp.stack(head_sums))


def attend_back(queries, key_rows, value_rows, attended, grad_att, logsums, segment, block_rows):
    grads_q = []
    grads_k = []
    grads_v = []
    for head_index in range(queries.shape[1] // 64):
        head_cols = slice(64 * head_index, 64 * head_index + 64)
        head_query = queries[:, head_cols]
        head_keys = key_rows[:, head_cols]
        head_values = value_rows[:, head_cols]
        head_grad = grad_att[:, head_cols]
        row_delta = jnp.sum(
            head_grad.astype(jnp.float32) * attended[:, head_cols].astype(jnp.float32), axis=1
        )
        scores = block_scores(head_query, head_keys, segment)
        prob_full = jnp.exp(scores - logsums[head_index, 0:block_rows][:, None])
        grad_v = contract_rows(prob_full.astype(jnp.bfloat16), head_grad)
        grad_p = contract_last(head_grad, head_values)
        grad_s = (prob_full * (grad_p - row_delta[0:block_rows, None])).astype(jnp.bfloat16)
        query_blocks = jnp.dot(grad_s, head_keys, preferred_element_type=jnp.float32) * score_scale
        grad_k = contract_rows(grad_s, head_query) * score_scale
        grads_q.append(query_blocks)
        grads_k.append(grad_k)
        grads_v.append(grad_v)
    return (
        jnp.concatenate(grads_q, axis=1),
        jnp.concatenate(grads_k, axis=1),
        jnp.concatenate(grads_v, axis=1),
    )


def swap(values, axis, bit):
    count = lax.axis_size(axis)
    return lax.ppermute(values, axis, [(i, i ^ bit) for i in range(count)])


def xor_order(blocks, index):
    step = 1
    while step < len(blocks):
        flip = (index // step) % 2 == 1
        blocks = [
            jnp.where(flip, blocks[place ^ step], blocks[place]) for place in range(len(blocks))
        ]
        step *= 2
    return blocks


def exchange_ctx(pieces):
    ctx_count = lax.axis_size("ctx")
    own = lax.axis_index("ctx")
    arrived = []
    for bit in range(ctx_count):
        piece = lax.dynamic_index_in_dim(pieces, own ^ bit, 0, keepdims=False)
        arrived.append(swap(piece, "ctx", bit) if bit else piece)
    return xor_order(arrived, own)


def gather_fsdp(block):
    count = lax.axis_size("fsdp")
    if count > 8:
        return lax.all_gather(block, "fsdp", axis=0, tiled=True)
    arrived = [None] * count
    for bit in range(0, count, 2):
        arrived[bit] = swap(block, "fsdp", bit) if bit else block
    for bit in range(0, count, 2):
        arrived[bit + 1] = swap(arrived[bit], "fsdp", 1)
    return jnp.concatenate(xor_order(arrived, lax.axis_index("fsdp")), axis=0)


def scatter_fsdp(rows):
    count = lax.axis_size("fsdp")
    blocks = rows.reshape(count, rows.shape[0] // count, rows.shape[1])
    if count > 8:
        return lax.psum_scatter(rows, "fsdp", scatter_dimension=0, tiled=True).astype(jnp.float32)
    own = lax.axis_index("fsdp")
    total = None
    order = [2 * (i % (count // 2)) for i in range(1, count // 2 + 1)]
    for bit in order:
        mine = lax.dynamic_index_in_dim(blocks, own ^ bit, 0, keepdims=False)
        other = lax.dynamic_index_in_dim(blocks, own ^ bit ^ 1, 0, keepdims=False)
        both = mine + swap(other, "fsdp", 1)
        if bit:
            both = swap(both, "fsdp", bit)
        total = both.astype(jnp.float32) if total is None else total + both.astype(jnp.float32)
    return total


def local(
    inputs,
    lengths,
    norm1_gain,
    qkv_weight,
    attn_out_weight,
    norm2_gain,
    ffn_in_weight,
    ffn_out_weight,
    out_grad,
):
    f32 = jnp.float32
    bf16 = jnp.bfloat16
    tok_dev = inputs.shape[0]
    width = inputs.shape[1]
    ctx_count = lax.axis_size("ctx")
    own = lax.axis_index("ctx")
    core = own % 2
    part = width // ctx_count
    part_heads = part // 64
    group_rows = tok_dev * ctx_count
    shard_rows = qkv_weight.shape[0]
    hidden = ffn_out_weight.shape[0]
    hid = hidden // ctx_count

    def by_part(weight, copies):
        split = weight.reshape(shard_rows, copies, ctx_count, -1)
        return split.transpose(2, 0, 1, 3).reshape(ctx_count, shard_rows, -1)

    gains = jnp.stack([norm1_gain, norm2_gain], axis=1)
    first = jnp.concatenate(
        [
            by_part(qkv_weight, 3),
            jnp.broadcast_to(
                jnp.pad(gains, ((0, 0), (0, 62)))[None], (ctx_count, shard_rows, 64)
            ),
        ],
        axis=2,
    )
    second = jnp.concatenate(
        [by_part(ffn_in_weight, 2), by_part(ffn_out_weight.T, 1), by_part(attn_out_weight, 1)],
        axis=2,
    )
    first_all = gather_fsdp(jnp.concatenate(exchange_ctx(first), axis=0))
    both_rows = jnp.concatenate([inputs, out_grad], axis=1)
    both_rows = lax.all_gather(both_rows, "ctx", axis=0, tiled=True)
    rows_in = both_rows[:, :width]
    rows_grad = both_rows[:, width:]
    second_all = gather_fsdp(jnp.concatenate(exchange_ctx(second), axis=0))
    w_qkv = first_all[:, : 3 * part]
    gain_one = first_all[:, 3 * part].astype(f32)
    gain_two = first_all[:, 3 * part + 1].astype(f32)
    w_in = second_all[:, : 2 * hid]
    w_out_t = second_all[:, 2 * hid : 3 * hid]
    w_attn_part = second_all[:, 3 * hid :]
    w_attn = jnp.concatenate(
        xor_order(
            [w_attn_part] + [swap(w_attn_part, "ctx", bit) for bit in range(1, ctx_count)], own
        ),
        axis=1,
    )

    index_rows = jnp.arange(group_rows, dtype=jnp.int32)
    segment, places = positions(lengths[0], index_rows)
    cosine, sine_tab = rope_tables(places)
    resid_in = rows_in.astype(f32)
    normed_one, scale_one = layer_norm(resid_in)
    hidden_one = (normed_one * gain_one).astype(bf16)
    joined_out = jnp.dot(hidden_one, w_qkv, preferred_element_type=f32)

    def heads(cols):
        return cols.reshape(group_rows, part_heads, 64)

    queries = rotate(heads(joined_out[:, :part]), cosine, sine_tab)
    queries = queries.reshape(group_rows, part).astype(bf16)
    key_rows = rotate(heads(joined_out[:, part : 2 * part]), cosine, sine_tab)
    key_rows = key_rows.reshape(group_rows, part).astype(bf16)
    value_rows = joined_out[:, 2 * part :].astype(bf16)
    att_part, logsums = attend(queries, key_rows, value_rows, segment, group_rows)
    attended = lax.all_gather(att_part, "ctx", axis=1, tiled=True)

    resid_mid = resid_in + jnp.dot(attended, w_attn, preferred_element_type=f32)
    normed_two, scale_two = layer_norm(resid_mid)
    hidden_two = (normed_two * gain_two).astype(bf16)
    expanded = jnp.dot(hidden_two, w_in, preferred_element_type=f32)
    gate_in = expanded[:, :hid]
    up_in = expanded[:, hid:]
    activated, gelu_slope = gelu_parts(gate_in)
    mixed_act = (activated * up_in).astype(bf16)
    out_part = contract_last(mixed_act, w_out_t).astype(bf16)
    grad_mixed = jnp.dot(rows_grad, w_out_t, preferred_element_type=f32)
    grad_expanded = jnp.concatenate(
        [grad_mixed * up_in * gelu_slope, grad_mixed * activated], axis=1
    ).astype(bf16)
    grad_hidden_two = contract_last(grad_expanded, w_in)
    grad_gain_two = jnp.sum(grad_hidden_two * normed_two, axis=0)

    def halves(rows):
        return rows.reshape(ctx_count // 2, 2, tok_dev, -1)

    def pair_sum(rows):
        split = halves(rows)
        mine = lax.dynamic_index_in_dim(split, core, 1, keepdims=False)
        other = lax.dynamic_index_in_dim(split, 1 - core, 1, keepdims=False)
        return mine.astype(f32) + swap(other, "ctx", 1).astype(f32)

    def own_rows(pair):
        return lax.dynamic_index_in_dim(pair, own // 2, 0, keepdims=False)

    def scatter_ctx(rows):
        pair = pair_sum(rows)
        mine = own_rows(pair)
        other = lax.dynamic_index_in_dim(pair, 1 - own // 2, 0, keepdims=False)
        return mine + swap(other.astype(bf16), "ctx", 2).astype(f32)

    pair = pair_sum(grad_hidden_two.astype(bf16))
    grad_h2_half = pair + swap(pair.astype(bf16), "ctx", 2).astype(f32)

    def my_half(rows):
        return lax.dynamic_index_in_dim(halves(rows), core, 1, keepdims=False)

    grad_mid_half = my_half(rows_grad).astype(f32) + norm_back(
        grad_h2_half, my_half(normed_two), my_half(scale_two), gain_two
    )
    half_bf = grad_mid_half.astype(bf16)
    other_bf = swap(half_bf, "ctx", 1)
    grad_mid = jnp.stack(xor_order([half_bf, other_bf], core), axis=1).reshape(group_rows, width)
    w_attn_rows = lax.dynamic_slice_in_dim(w_attn, own * part, part, 0)
    grad_att = contract_last(grad_mid, w_attn_rows).astype(bf16)

    second_sum = scatter_fsdp(
        jnp.concatenate(
            [
                contract_rows(hidden_two, grad_expanded),
                contract_rows(rows_grad, mixed_act),
                contract_rows(attended, lax.dynamic_slice_in_dim(grad_mid, own * part, part, 1)),
            ],
            axis=1,
        ).astype(bf16)
    )
    out_own = scatter_ctx(out_part)
    outputs = (own_rows(my_half(resid_mid)) + out_own).astype(bf16)

    grad_q, grad_k, grad_v = attend_back(
        queries, key_rows, value_rows, att_part, grad_att, logsums, segment, group_rows
    )
    grad_q = unrotate(heads(grad_q), cosine, sine_tab).reshape(group_rows, part)
    grad_k = unrotate(heads(grad_k), cosine, sine_tab).reshape(group_rows, part)
    grad_joined = jnp.concatenate([grad_q, grad_k, grad_v], axis=1).astype(bf16)
    grad_hidden_one = contract_last(grad_joined, w_qkv)
    grad_gain_one = jnp.sum(grad_hidden_one * normed_one, axis=0)
    first_sum = scatter_fsdp(
        jnp.concatenate(
            [
                contract_rows(hidden_one, grad_joined),
                grad_gain_one[:, None],
                grad_gain_two[:, None],
                jnp.zeros((width, 62), f32),
            ],
            axis=1,
        ).astype(bf16)
    )
    grad_h1_own = scatter_ctx(grad_hidden_one.astype(bf16))
    input_grad = (
        own_rows(grad_mid_half)
        + norm_back(
            grad_h1_own, own_rows(my_half(normed_one)), own_rows(my_half(scale_one)), gain_one
        )
    ).astype(bf16)

    second_own = exchange_ctx(second_sum.astype(bf16).reshape(ctx_count, shard_rows, -1))
    first_own = exchange_ctx(first_sum.astype(bf16).reshape(ctx_count, shard_rows, -1))
    second_own = jnp.stack([v.astype(f32) for v in second_own], axis=1)
    first_own = jnp.stack([v.astype(f32) for v in first_own], axis=1)

    def whole(cols, copies):
        split = cols.reshape(shard_rows, ctx_count, copies, -1)
        return split.transpose(0, 2, 1, 3).reshape(shard_rows, -1)

    return (
        outputs,
        input_grad,
        jnp.sum(first_own[:, :, 3 * part], axis=1),
        whole(first_own[:, :, : 3 * part], 3),
        whole(second_own[:, :, 3 * hid :], 1),
        jnp.sum(first_own[:, :, 3 * part + 1], axis=1),
        whole(second_own[:, :, : 2 * hid], 2),
        whole(second_own[:, :, 2 * hid : 3 * hid], 1).T,
    )


def solution(mesh):
    in_specs = (
        P(("fsdp", "ctx"), None),
        P("fsdp", None),
        P(("fsdp", "ctx")),
        P(("fsdp", "ctx"), None),
        P(("fsdp", "ctx"), None),
        P(("fsdp", "ctx")),
        P(("fsdp", "ctx"), None),
        P(None, ("fsdp", "ctx")),
        P(("fsdp", "ctx"), None),
    )
    out_specs = (
        P(("fsdp", "ctx"), None),
        P(("fsdp", "ctx"), None),
        P(("fsdp", "ctx")),
        P(("fsdp", "ctx"), None),
        P(("fsdp", "ctx"), None),
        P(("fsdp", "ctx")),
        P(("fsdp", "ctx"), None),
        P(None, ("fsdp", "ctx")),
    )
    return jax.shard_map(local, mesh=mesh, in_specs=in_specs, out_specs=out_specs, check_vma=False)
```
